32 devices in a mesh: dp: 4 (over z), rows: 4 (over y, core), cols: 2 (over x).
Axes of the slice: x: 2, y: 2, z: 4, core: 2. Of those that a mesh axis runs over, the one named last changes fastest.
Arguments:
- hidden_in: bfloat16 [3072, 1536], P(('dp', 'cols'), 'rows'), may hold values from -7 to 7
- attn_gain: float32 [2, 1536], P(None, 'rows'), may hold values from 0.1 to 1.9
- w_qkv: bfloat16 [2, 1536, 2048], P(None, 'rows', 'cols'), may hold values from -0.15625 to 0.15625
- b_qkv: float32 [2, 2048], P(None, 'cols'), may hold values from -2 to 2
- w_out: bfloat16 [2, 1536, 1536], P(None, 'cols', 'rows'), may hold values from -0.3125 to 0.3125
- mlp_gain: float32 [2, 1536], P(None, 'rows'), may hold values from 0.1 to 1.9
- w_gate: bfloat16 [2, 1536, 8960], P(None, 'rows', 'cols'), may hold values from -0.15625 to 0.15625
- w_up: bfloat16 [2, 1536, 8960], P(None, 'rows', 'cols'), may hold values from -0.15625 to 0.15625
- w_down: bfloat16 [2, 8960, 1536], P(None, 'cols', 'rows'), may hold values from -0.0625 to 0.0625
- out_grad: bfloat16 [3072, 1536], P(('dp', 'cols'), 'rows'), may hold values from -6 to 6
Outputs:
- hidden_out: bfloat16 [3072, 1536], P(('dp', 'cols'), 'rows')
- in_grad: float32 [3072, 1536], P(('dp', 'cols'), 'rows')
- attn_gain_grad: float32 [2, 1536], P(None, 'rows')
- w_qkv_grad: float32 [2, 1536, 2048], P(None, 'rows', 'cols')
- b_qkv_grad: float32 [2, 2048], P(None, 'cols')
- w_out_grad: float32 [2, 1536, 1536], P(None, 'cols', 'rows')
- mlp_gain_grad: float32 [2, 1536], P(None, 'rows')
- w_gate_grad: float32 [2, 1536, 8960], P(None, 'rows', 'cols')
- w_up_grad: float32 [2, 1536, 8960], P(None, 'rows', 'cols')
- w_down_grad: float32 [2, 8960, 1536], P(None, 'cols', 'rows')
The draws below stay inside these ranges and needn't reach their ends.
All inputs are finite; a program needn't handle non-finite values.
Results may differ from the reference program's by a relative error of at most 0.025.
Values may be sent and summed in bfloat16 or wider, within the bound.
No kernel may reach another device: no remote copies, remote signals or barrier semaphores. Data moves between devices by JAX's collectives and lax.ppermute only.
A program may use at most 320 MiB of HBM per device.

```python
import jax
import jax.numpy as jnp
from jax import lax

D = 1536
HEADS = 12
KV_HEADS = 2
HEAD_DIM = 128
FF = 8960
SEQ = 192
LAYERS = 2
TOK_GROUP = 768
TOKENS = 3072
QKV = 2048
HQD = 1536
N_DP = 4


def draw_hidden_in(key, part):
    noise_key = jax.random.fold_in(key, 11)
    column = jnp.arange(D, dtype=jnp.float32)
    column_scale = 0.5 + 1.5 * column / D
    base_values = jax.random.truncated_normal(noise_key, -3.0, 3.0, (TOKENS, D), jnp.float32)
    return (base_values * column_scale[None, :]).astype(jnp.bfloat16)


def level_of(rng, extent, split, least, largest):
    gain, own = 1.0, jax.random.fold_in(rng, 6)
    for dim, blocks in split:
        heights = jnp.exp(jax.random.uniform(jax.random.fold_in(own, dim), (blocks,), jnp.float32, least / len(split), largest / len(split)))
        gain = gain * jnp.repeat(heights, extent[dim] // blocks).reshape([-1 if axis == dim else 1 for axis in range(len(extent))])
    return gain


def centred(rng, dims, deviation, limit, split=(), kind=jnp.bfloat16):
    values = deviation * jax.random.normal(rng, dims, jnp.float32)
    if split:
        values = values * level_of(rng, dims, split, -0.22, 0.18)
    return jnp.clip(values, -limit, limit).astype(kind)


def setup_inputs(seed: int = 0) -> dict:
    key_list = jax.random.split(jax.random.key(seed), 11)
    hidden_in = draw_hidden_in(jax.random.fold_in(key_list[10], 71), 0)
    attn_gain = jnp.clip(1.0 + 0.18 * jax.random.normal(key_list[1], (LAYERS, D), jnp.float32), 0.1, 1.9)
    w_qkv = centred(key_list[2], (LAYERS, D, QKV), D ** -0.5, 0.15625, ((1, 4), (2, 2)))
    b_qkv = centred(key_list[3], (LAYERS, QKV), 0.5, 2.0, ((1, 2),), jnp.float32)
    w_out = centred(key_list[4], (LAYERS, HQD, D), (HQD // 4) ** -0.5, 0.3125, ((1, 2), (2, 4)))
    mlp_gain = jnp.clip(1.0 + 0.18 * jax.random.normal(key_list[5], (LAYERS, D), jnp.float32), 0.1, 1.9)
    w_gate = centred(key_list[6], (LAYERS, D, FF), D ** -0.5, 0.15625, ((1, 4), (2, 2)))
    w_up = centred(key_list[7], (LAYERS, D, FF), D ** -0.5, 0.15625, ((1, 4), (2, 2)))
    w_down = centred(key_list[8], (LAYERS, FF, D), FF ** -0.5, 0.0625, ((1, 2), (2, 4)))
    out_grad = centred(key_list[9], (TOKENS, D), 1.0, 6.0, ((0, 8), (1, 4)))
    return dict(hidden_in=hidden_in, attn_gain=attn_gain, w_qkv=w_qkv, b_qkv=b_qkv, w_out=w_out, mlp_gain=mlp_gain, w_gate=w_gate, w_up=w_up, w_down=w_down, out_grad=out_grad)


eps = 1e-06
theta = 1000000.0
masked = -1e+30

def rotate_half(values):
    half_dim = values.shape[-1] // 2
    return jnp.concatenate([-values[..., half_dim:], values[..., :half_dim]], axis=-1)

def rope_tables():
    frequency = theta ** (-jnp.arange(0, HEAD_DIM, 2, dtype=jnp.float32) / HEAD_DIM)
    angles = jnp.arange(SEQ, dtype=jnp.float32)[:, None] * frequency[None, :]
    angles = jnp.concatenate([angles, angles], axis=-1)
    return (jnp.cos(angles), jnp.sin(angles))

def causal_scores(query_round, key_round):
    raw_scores = jnp.einsum('sikgd,sjkd->skgij', query_round.astype(jnp.float32), key_round.astype(jnp.float32)) * HEAD_DIM ** (-0.5)
    position = jnp.arange(SEQ)
    return jnp.where(position[:, None] >= position[None, :], raw_scores, masked)

def attention_forward(qkv_rows, kv_count, group_size):
    blocks = qkv_rows.reshape(-1, SEQ, kv_count, group_size + 2, HEAD_DIM)
    cosine, sine_table = rope_tables()
    query = blocks[:, :, :, :group_size]
    key_part = blocks[:, :, :, group_size]
    value_part = blocks[:, :, :, group_size + 1]
    query = query * cosine[None, :, None, None, :] + rotate_half(query) * sine_table[None, :, None, None, :]
    key_part = key_part * cosine[None, :, None, :] + rotate_half(key_part) * sine_table[None, :, None, :]
    query_round = query.astype(jnp.bfloat16)
    key_round = key_part.astype(jnp.bfloat16)
    value_round = value_part.astype(jnp.bfloat16)
    scores = causal_scores(query_round, key_round)
    highest = lax.optimization_barrier(jnp.max(scores, axis=-1, keepdims=True))
    log_total = highest + jnp.log(lax.optimization_barrier(jnp.sum(jnp.exp(scores - highest), axis=-1, keepdims=True)))
    weights_round = jnp.exp(scores - log_total).astype(jnp.bfloat16)
    attended = jnp.einsum('skgij,sjkd->sikgd', weights_round.astype(jnp.float32), value_round.astype(jnp.float32))
    attended = attended.astype(jnp.bfloat16).reshape(qkv_rows.shape[0], -1)
    return (attended, (query_round, key_round, value_round, log_total))

def attention_backward(grad_attended, attn_kept, kv_count, group_size):
    query_round, key_round, value_round, log_total = attn_kept
    grad_round = grad_attended.astype(jnp.bfloat16).reshape(-1, SEQ, kv_count, group_size, HEAD_DIM)
    grad_wide = grad_round.astype(jnp.float32)
    scores = causal_scores(query_round, key_round)
    prob_full = jnp.exp(scores - log_total)
    weights_round = prob_full.astype(jnp.bfloat16)
    grad_value = jnp.einsum('skgij,sikgd->sjkd', weights_round.astype(jnp.float32), grad_wide)
    grad_prob = jnp.einsum('sikgd,sjkd->skgij', grad_wide, value_round.astype(jnp.float32))
    grad_scores = prob_full * (grad_prob - lax.optimization_barrier(jnp.sum(prob_full * grad_prob, axis=-1, keepdims=True))) * HEAD_DIM ** (-0.5)
    grad_scores = grad_scores.astype(jnp.bfloat16).astype(jnp.float32)
    grad_query = jnp.einsum('skgij,sjkd->sikgd', grad_scores, key_round.astype(jnp.float32))
    grad_key = jnp.einsum('skgij,sikgd->sjkd', grad_scores, query_round.astype(jnp.float32))
    cosine, sine_table = rope_tables()
    grad_query = grad_query * cosine[None, :, None, None, :] - rotate_half(grad_query) * sine_table[None, :, None, None, :]
    grad_key = grad_key * cosine[None, :, None, :] - rotate_half(grad_key) * sine_table[None, :, None, :]
    joined = jnp.concatenate([grad_query, grad_key[:, :, :, None], grad_value[:, :, :, None]], axis=3)
    return joined.reshape(grad_attended.shape[0], -1)

def norm_forward(resid, gain_row):
    scale_row = lax.rsqrt(lax.optimization_barrier(jnp.mean(resid * resid, axis=1)) + eps)
    normed = (resid * scale_row[:, None] * gain_row[None, :]).astype(jnp.bfloat16)
    return (normed, scale_row)

def norm_backward(grad_normed, resid, scale_row, gain_row):
    scaled = grad_normed * gain_row[None, :]
    inner = lax.optimization_barrier(jnp.sum(scaled * resid, axis=1))
    gain_grad = lax.optimization_barrier(jnp.sum(grad_normed * resid * scale_row[:, None], axis=0))
    grad_resid = scale_row[:, None] * scaled - resid * (scale_row * scale_row * scale_row * inner / D)[:, None]
    return (grad_resid, gain_grad)

def product(left, right):
    return jnp.dot(left, right, preferred_element_type=jnp.float32)

def run_group(tokens, cotangent, weights):
    attn_gain, w_qkv, b_qkv, w_out, mlp_gain, w_gate, w_up, w_down = weights
    group_size = HEADS // KV_HEADS
    resid = tokens.astype(jnp.float32)
    saved = []
    for which_layer in range(LAYERS):
        normed_attn, scale_attn = norm_forward(resid, attn_gain[which_layer])
        qkv_rows = product(normed_attn, w_qkv[which_layer]) + b_qkv[which_layer][None, :]
        attended, attn_kept = attention_forward(qkv_rows, KV_HEADS, group_size)
        middle = resid + product(attended, w_out[which_layer])
        normed_mlp, scale_mlp = norm_forward(middle, mlp_gain[which_layer])
        gate_proj = product(normed_mlp, w_gate[which_layer])
        up_proj = product(normed_mlp, w_up[which_layer])
        activated = (jax.nn.silu(gate_proj) * up_proj).astype(jnp.bfloat16)
        saved.append((resid, scale_attn, normed_attn, attn_kept, attended, middle, scale_mlp, normed_mlp, gate_proj, up_proj, activated))
        resid = middle + product(activated, w_down[which_layer])
    block_out = resid.astype(jnp.bfloat16)
    grad_resid = cotangent.astype(jnp.float32)
    layer_grads = [None] * LAYERS
    for which_layer in reversed(range(LAYERS)):
        resid, scale_attn, normed_attn, attn_kept, attended, middle, scale_mlp, normed_mlp, gate_proj, up_proj, activated = saved[which_layer]
        grad_round = grad_resid.astype(jnp.bfloat16)
        down_grad = product(activated.T, grad_round)
        grad_units = product(grad_round, w_down[which_layer].T)
        sigmoid_gate = jax.nn.sigmoid(gate_proj)
        grad_gate = (grad_units * up_proj * sigmoid_gate * (1.0 + gate_proj * (1.0 - sigmoid_gate))).astype(jnp.bfloat16)
        grad_up = (grad_units * gate_proj * sigmoid_gate).astype(jnp.bfloat16)
        gate_grad = product(normed_mlp.T, grad_gate)
        up_grad = product(normed_mlp.T, grad_up)
        grad_normed_mlp = product(grad_gate, w_gate[which_layer].T) + product(grad_up, w_up[which_layer].T)
        grad_inner, mlp_gain_part = norm_backward(grad_normed_mlp, middle, scale_mlp, mlp_gain[which_layer])
        grad_middle = grad_resid + grad_inner
        middle_round = grad_middle.astype(jnp.bfloat16)
        out_weight_grad = product(attended.T, middle_round)
        grad_heads = product(middle_round, w_out[which_layer].T)
        grad_qkv = attention_backward(grad_heads, attn_kept, KV_HEADS, group_size)
        bias_part = lax.optimization_barrier(jnp.sum(grad_qkv, axis=0))
        qkv_round = grad_qkv.astype(jnp.bfloat16)
        qkv_weight_grad = product(normed_attn.T, qkv_round)
        grad_normed_attn = product(qkv_round, w_qkv[which_layer].T)
        grad_first, attn_gain_part = norm_backward(grad_normed_attn, resid, scale_attn, attn_gain[which_layer])
        grad_resid = grad_middle + grad_first
        layer_grads[which_layer] = (attn_gain_part, qkv_weight_grad, bias_part, out_weight_grad, mlp_gain_part, gate_grad, up_grad, down_grad)
    stacked = tuple((jnp.stack([layer_grads[which_layer][member] for which_layer in range(LAYERS)]) for member in range(8)))
    return (block_out, grad_resid, stacked)

def reference(hidden_in, attn_gain, w_qkv, b_qkv, w_out, mlp_gain, w_gate, w_up, w_down, out_grad):
    weights = (attn_gain, w_qkv, b_qkv, w_out, mlp_gain, w_gate, w_up, w_down)
    inputs = (hidden_in.reshape(N_DP, TOK_GROUP, D), out_grad.reshape(N_DP, TOK_GROUP, D))
    initial = tuple((jnp.zeros(member.shape, jnp.float32) for member in weights))

    def group_step(totals, pair_block):
        block_out, block_grad, grads = run_group(pair_block[0], pair_block[1], weights)
        return (tuple((earlier + current for earlier, current in zip(totals, grads))), (block_out, block_grad))
    totals, (outputs, in_grads) = lax.scan(group_step, initial, inputs)
    return (outputs.reshape(TOKENS, D), in_grads.reshape(TOKENS, D), totals[0], totals[1], totals[2], totals[3], totals[4], totals[5], totals[6], totals[7])
```

```python
import jax
import jax.numpy as jnp
import numpy as np
from jax import lax
from jax.experimental import pallas as pl
from jax.experimental.pallas import tpu as pltpu
from jax.sharding import Mesh, PartitionSpec as P

D = 1536
HEADS = 12
KV_HEADS = 2
HEAD_DIM = 128
SEQ = 192
LAYERS = 2
QKV = 2048
GROUP = HEADS // KV_HEADS

eps = 1e-06
theta = 1000000.0
masked = -1e30


DP, RY, RK, CX = "dp", "ry", "rk", "cols"
ROWS = (RY, RK)
PLANE = (RY, CX)

f32 = jnp.float32
bf16 = jnp.bfloat16


def mm(left, right):
    return jnp.dot(left, right, preferred_element_type=f32)


def mm_t(left, right):
    return lax.dot_general(left, right, (((1,), (1,)), ((), ())), preferred_element_type=f32)


def t_mm(left, right):
    return lax.dot_general(left, right, (((0,), (0,)), ((), ())), preferred_element_type=f32)


def swap_core(values):
    return lax.ppermute(values, RK, [(0, 1), (1, 0)])


def swap_diagonal(values):
    return lax.ppermute(values, (RK, CX), [(0, 0), (1, 2), (2, 1), (3, 3)])


def swap_x(values):
    return lax.ppermute(values, CX, [(0, 1), (1, 0)])


def swap_y(values):
    return lax.ppermute(values, RY, [(0, 1), (1, 0)])


def gather_eight(values):
    half = values.shape[0] // 2
    by_x = swap_x(values)
    by_y = swap_y(values)
    first = swap_x(by_y[:half])
    second = swap_y(by_x[half:])
    near = jnp.concatenate([values, by_x, by_y, first, second], axis=0)
    return jnp.concatenate([near, swap_core(near)], axis=0)


def scatter_eight(partial):
    rows = partial.shape[0] // 8
    half = rows // 2
    other = swap_core(partial[4 * rows :].astype(bf16))
    summed = partial[: 4 * rows] + other.astype(f32)
    own, to_x, to_y, corner = (summed[i * rows : (i + 1) * rows] for i in range(4))
    corner = corner.astype(bf16)
    via_x = swap_x(corner[:half]).astype(f32)
    via_y = swap_y(corner[half:]).astype(f32)
    to_y = jnp.concatenate([to_y[:half] + via_x, to_y[half:]], axis=0).astype(bf16)
    to_x = jnp.concatenate([to_x[:half], to_x[half:] + via_y], axis=0).astype(bf16)
    return own + swap_x(to_x).astype(f32) + swap_y(to_y).astype(f32)


def rope_tables():
    frequency = theta ** (-np.arange(0, HEAD_DIM, 2, dtype=np.float32) / np.float32(HEAD_DIM))
    angles = np.arange(SEQ, dtype=np.float32)[:, None] * frequency[None, :].astype(np.float32)
    angles = np.concatenate([angles, angles], axis=-1).astype(np.float32)
    return np.cos(angles).astype(np.float32), np.sin(angles).astype(np.float32)


def rotate_half(values):
    half_dim = values.shape[-1] // 2
    return jnp.concatenate([-values[..., half_dim:], values[..., :half_dim]], axis=-1)


def attention_frame():
    second = lax.axis_index(RK) == 1
    cosine, sine = rope_tables()
    half = SEQ // 2
    cosine = jnp.where(second, np.roll(cosine, -half, axis=0), cosine)
    sine = jnp.where(second, np.roll(sine, -half, axis=0), sine)
    position = (jnp.arange(SEQ) + half * lax.axis_index(RK)) % SEQ
    mask = position[:, None] >= position[None, :]
    return cosine, sine, mask


def causal_scores(query_round, key_round, mask):
    raw_scores = jnp.einsum("igd,jd->gij", query_round, key_round, preferred_element_type=f32)
    return jnp.where(mask[None], raw_scores * HEAD_DIM ** (-0.5), masked)


def attention_forward(qkv_rows, frame):
    cosine, sine, mask = frame
    blocks = qkv_rows.reshape(SEQ, GROUP + 2, HEAD_DIM)
    turned = blocks[:, : GROUP + 1]
    turned = turned * cosine[:, None, :] + rotate_half(turned) * sine[:, None, :]
    turned = turned.astype(bf16)
    query_round = turned[:, :GROUP]
    key_round = turned[:, GROUP]
    value_round = blocks[:, GROUP + 1].astype(bf16)
    scores = causal_scores(query_round, key_round, mask)
    highest = jnp.max(scores, axis=-1, keepdims=True)
    log_total = highest + jnp.log(jnp.sum(jnp.exp(scores - highest), axis=-1, keepdims=True))
    weights_round = jnp.exp(scores - log_total).astype(bf16)
    attended = jnp.einsum("gij,jd->igd", weights_round, value_round, preferred_element_type=f32)
    attended = attended.astype(bf16).reshape(SEQ, -1)
    return attended, (query_round, key_round, value_round, log_total)


def attention_backward(grad_attended, kept, frame):
    cosine, sine, mask = frame
    query_round, key_round, value_round, log_total = kept
    grad_round = grad_attended.astype(bf16).reshape(SEQ, GROUP, HEAD_DIM)
    scores = causal_scores(query_round, key_round, mask)
    prob = jnp.exp(scores - log_total)
    weights_round = prob.astype(bf16)
    grad_value = jnp.einsum("gij,igd->jd", weights_round, grad_round, preferred_element_type=f32)
    grad_prob = jnp.einsum("igd,jd->gij", grad_round, value_round, preferred_element_type=f32)
    inner = jnp.sum(prob * grad_prob, axis=-1, keepdims=True)
    grad_scores = (prob * (grad_prob - inner) * HEAD_DIM ** (-0.5)).astype(bf16)
    grad_query = jnp.einsum("gij,jd->igd", grad_scores, key_round, preferred_element_type=f32)
    grad_key = jnp.einsum("gij,igd->jd", grad_scores, query_round, preferred_element_type=f32)
    turned = jnp.concatenate([grad_query, grad_key[:, None]], axis=1)
    turned = turned * cosine[:, None, :] - rotate_half(turned) * sine[:, None, :]
    joined = jnp.concatenate([turned, grad_value[:, None]], axis=1)
    return joined.reshape(SEQ, -1)


def norm_forward(resid, gain_row):
    scale_row = lax.rsqrt(jnp.mean(resid * resid, axis=1) + eps)
    normed = (resid * scale_row[:, None] * gain_row[None, :]).astype(bf16)
    return normed, scale_row


def norm_backward(grad_normed, resid, scale_row, gain_row):
    scaled = grad_normed * gain_row[None, :]
    inner = jnp.sum(scaled * resid, axis=1)
    gain_grad = jnp.sum(grad_normed * resid * scale_row[:, None], axis=0)
    grad_resid = (
        scale_row[:, None] * scaled
        - resid * (scale_row * scale_row * scale_row * inner / D)[:, None]
    )
    return grad_resid, gain_grad


def sum_dp(values):
    summed = lax.psum_scatter(values, DP, scatter_dimension=0, tiled=True)
    return lax.all_gather(summed, DP, axis=0, tiled=True)


def xor_permute(values, bits):
    return lax.ppermute(values, ROWS, [(i, i ^ bits) for i in range(4)])


def swap_group(values):
    count = lax.axis_size(DP)
    return lax.ppermute(values, DP, [(i, i ^ 1) for i in range(count)])


def take(arrays, scalars, layer, grid, block, place, out_shape, bound_dim, bound):
    count = len(arrays)
    rows, width = block

    def kernel(scalar_ref, *refs):
        out_ref = refs[count]
        step = pl.program_id(0)
        first = place(step, scalar_ref)[bound_dim] * block[bound_dim]
        if bound is not None:
            index = lax.broadcasted_iota(jnp.int32, (rows, width), bound_dim) + first
        for i in range(count):
            values = refs[i][...].reshape(rows, width)
            if bound is not None:
                values = jnp.where(index < bound, values, jnp.zeros_like(values))
            out_ref[i] = values

    if layer is None:
        in_specs = [pl.BlockSpec(block, lambda i, s: place(i, s))] * count
    else:
        in_specs = [pl.BlockSpec((1, *block), lambda i, s: (layer, *place(i, s)))] * count
    along = 0 if out_shape[1] == width else 1
    out_map = (lambda i, s: (0, i, 0)) if along == 0 else (lambda i, s: (0, 0, i))
    return pl.pallas_call(
        kernel,
        grid_spec=pltpu.PrefetchScalarGridSpec(
            num_scalar_prefetch=1,
            grid=(grid,),
            in_specs=in_specs,
            out_specs=pl.BlockSpec((count, rows, width), out_map),
        ),
        out_shape=jax.ShapeDtypeStruct((count, *out_shape), arrays[0].dtype),
    )(scalars, *arrays)


def join(parts, scalars, block, place, out_shape, dtype, layer=None, into=None):
    count = parts[0].shape[0]
    rows, width = block
    tiles = parts[0].shape[2] // width

    def kernel(scalar_ref, *refs):
        outs = refs[len(refs) - count :]
        piece = pl.program_id(0)
        for which, (low, high) in enumerate([(0, 1), (2, 3), (4, 4), (5, 5), (6, 6), (7, 7)]):

            @pl.when((piece >= low) & (piece <= high))
            def _():
                for i in range(count):
                    outs[i][...] = refs[which][i].astype(dtype).reshape(outs[i].shape)

    def part_map(low, high):
        def index(i, j, s):
            inside = (i >= low) & (i <= high)
            tile = jnp.where(inside, j, jnp.where(i < low, 0, tiles - 1))
            return 0, jnp.clip(i - low, 0, high - low), tile

        return index

    in_specs = [
        pl.BlockSpec((count, rows, width), part_map(low, high))
        for low, high in [(0, 1), (2, 3), (4, 4), (5, 5), (6, 6), (7, 7)]
    ]
    operands = list(parts)
    aliases = {}
    if into is not None:
        for i, buffer in enumerate(into):
            aliases[1 + len(operands)] = i
            operands.append(buffer)
            in_specs.append(pl.BlockSpec(memory_space=pl.ANY))
    if layer is None:
        out_spec = pl.BlockSpec(block, lambda i, j, s: place(i, j, s))
    else:
        out_spec = pl.BlockSpec((1, *block), lambda i, j, s: (layer, *place(i, j, s)))
    return pl.pallas_call(
        kernel,
        grid_spec=pltpu.PrefetchScalarGridSpec(
            num_scalar_prefetch=1,
            grid=(8, tiles),
            in_specs=in_specs,
            out_specs=[out_spec] * count,
        ),
        out_shape=[jax.ShapeDtypeStruct(out_shape, dtype)] * count,
        input_output_aliases=aliases,
    )(scalars, *operands)


def gated(gate, up, grad_units):
    sigmoid_gate = jax.nn.sigmoid(gate)
    activated = (gate * sigmoid_gate * up).astype(bf16)
    grad_gate = grad_units * up * sigmoid_gate * (1.0 + gate * (1.0 - sigmoid_gate))
    grad_up = grad_units * gate * sigmoid_gate
    return activated, grad_gate.astype(bf16), grad_up.astype(bf16)


def body(hidden_in, attn_gain, w_qkv, b_qkv, w_out, mlp_gain, w_gate, w_up, w_down, out_grad):
    units = w_gate.shape[2]
    share = -(-units // (4 * 128)) * 128
    extra = 4 * share - units
    core = lax.axis_index(RK)
    column = lax.axis_index(CX)
    frame = attention_frame()
    everyone = lax.axis_size(DP) <= 4

    place = lax.axis_index(RY) * 2 + core
    gains = lax.dynamic_update_slice(
        jnp.zeros((2 * LAYERS, D), f32),
        jnp.concatenate([attn_gain, mlp_gain], axis=0),
        (0, place * attn_gain.shape[1]),
    )
    gains = gains + swap_core(gains)
    gains = gains + swap_y(gains)
    attn_gain_full, mlp_gain_full = gains[:LAYERS], gains[LAYERS:]
    bias_other = swap_x(b_qkv)
    bias_here = jnp.where(core == column, b_qkv, bias_other)

    def tokens_whole(values):
        count, rows, width = values.shape
        blocks = values.reshape(count, 4, rows // 4, width)
        arrived = lax.all_to_all(blocks, ROWS, 1, 1, tiled=True)
        return jnp.concatenate([arrived[:, i] for i in range(4)], axis=-1)

    def features_back(values):
        rows, width = values.shape[0], values.shape[1] // 4
        blocks = jnp.stack([values[:, i * width : (i + 1) * width] for i in range(4)])
        return lax.all_to_all(blocks, ROWS, 0, 0, tiled=True).reshape(4 * rows, width)

    def fetch_attention(layer, earlier):
        qkv_near = swap_diagonal(after(w_qkv[layer], earlier))
        out_near = swap_diagonal(after(w_out[layer], qkv_near))
        qkv_block = lax.all_gather(qkv_near, PLANE, axis=0)
        out_block = lax.all_gather(out_near, PLANE, axis=0)
        qkv_full = qkv_block.reshape(D, -1)
        out_full = jnp.concatenate([out_block[i] for i in range(4)], axis=1)
        return qkv_full, out_full

    half_d = D // 8
    parity = lax.axis_index(DP) % 2
    sources = [place ^ bits for bits in range(4)]
    piece_source = [sources[i // 2] for i in range(8)]
    piece_half = [jnp.int32(0), jnp.int32(1)] * 2 + [parity, 1 - parity] * 2
    join_table = jnp.stack(piece_source + piece_half).astype(jnp.int32)

    def pairs_of(own_part, core_part, y_part, corner_part):
        y_mine = xor_permute(y_part, 2)
        corner_mine = xor_permute(corner_part, 3)
        return (
            own_part,
            swap_core(core_part),
            y_mine,
            swap_group(y_mine),
            corner_mine,
            swap_group(corner_mine),
        )

    def pick(block, half):
        return jnp.stack([block, half]).astype(jnp.int32)

    def after(value, earlier):
        return value if earlier is None else lax.optimization_barrier((value, earlier))[0]

    col_tile = share // 3
    unit_half = share // 2

    def fetch_wide(layer, earlier):
        def blocks(bits, rows):
            return take(
                (w_gate, w_up),
                after(pick(sources[bits], parity if rows == half_d else 0 * parity), earlier),
                layer,
                3,
                (rows, col_tile),
                lambda i, s: (s[1], 3 * s[0] + i),
                (rows, share),
                1,
                units,
            )

        parts = pairs_of(
            blocks(0, 2 * half_d), blocks(1, 2 * half_d), blocks(2, half_d), blocks(3, half_d)
        )
        return join(
            parts,
            join_table,
            (half_d, share),
            lambda i, j, s: (2 * s[i] + s[8 + i], 0),
            (D, share),
            bf16,
        )

    def fetch_narrow(layer, earlier):
        def blocks(bits, count):
            return take(
                (w_down,),
                after(pick(sources[bits], parity if count == 1 else 0 * parity), earlier),
                layer,
                count,
                (unit_half, D // 4),
                lambda i, s: (2 * s[0] + s[1] + i, 0),
                (count * unit_half, D // 4),
                0,
                units,
            )

        parts = pairs_of(blocks(0, 2), blocks(1, 2), blocks(2, 1), blocks(3, 1))
        return join(
            parts,
            join_table,
            (unit_half, D // 4),
            lambda i, j, s: (s[8 + i], s[i]),
            (share, D),
            bf16,
        )[0]

    def give_wide(grads, layer, into):
        def blocks(bits, rows):
            return take(
                grads,
                pick(sources[bits], parity if rows == half_d else 0 * parity),
                None,
                1,
                (rows, share),
                lambda i, s: (s[0] * (2 * half_d // rows) + s[1], 0),
                (rows, share),
                1,
                None,
            )

        parts = pairs_of(
            blocks(0, 2 * half_d), blocks(1, 2 * half_d), blocks(2, half_d), blocks(3, half_d)
        )
        return join(
            parts,
            join_table,
            (half_d, col_tile),
            lambda i, j, s: (s[8 + i], 3 * s[i] + j),
            w_gate.shape,
            f32,
            layer,
            into,
        )

    def give_narrow(grad, layer, into):
        def blocks(bits, count):
            return take(
                (grad,),
                pick(sources[bits], parity if count == 1 else 0 * parity),
                None,
                count,
                (unit_half, D // 4),
                lambda i, s: (s[1] + i, s[0]),
                (count * unit_half, D // 4),
                0,
                None,
            )

        parts = pairs_of(blocks(0, 2), blocks(1, 2), blocks(2, 1), blocks(3, 1))
        return join(
            parts,
            join_table,
            (unit_half, D // 4),
            lambda i, j, s: (2 * s[i] + s[8 + i], 0),
            w_down.shape,
            f32,
            layer,
            into,
        )

    def return_wide(grad):
        blocks = grad.astype(bf16).reshape(4, D // 4, share)
        arrived = lax.all_to_all(blocks, ROWS, 0, 0, tiled=True)
        spread = jnp.concatenate([arrived[i] for i in range(4)], axis=1)[:, :units]
        return sum_dp(spread)

    def return_narrow(grad):
        rows = grad.astype(bf16)
        blocks = jnp.stack([rows[:, i * (D // 4) : (i + 1) * (D // 4)] for i in range(4)])
        arrived = lax.all_to_all(blocks, ROWS, 0, 0, tiled=True)
        spread = arrived.reshape(4 * share, -1)[:units]
        return sum_dp(spread)

    def return_qkv(grad):
        blocks = grad.astype(bf16).reshape(4, D // 4, -1)
        return sum_dp(swap_diagonal(lax.psum_scatter(blocks, PLANE)))

    def return_out(grad):
        rows = grad.astype(bf16)
        blocks = jnp.stack([rows[:, i * (D // 4) : (i + 1) * (D // 4)] for i in range(4)])
        return sum_dp(swap_diagonal(lax.psum_scatter(blocks, PLANE)))

    def all_tokens(values):
        if not everyone:
            return (values,)
        near = lax.all_gather(values[: values.shape[0] // 2], DP, axis=0, tiled=True)
        return near, swap_core(near)

    def mlp_weight_grads(inputs, cotangents, gate_w, up_w, down_w):
        totals = [0.0, 0.0, 0.0]
        for normed, grad in zip(inputs, cotangents):
            gate = mm(normed, gate_w)
            up = mm(normed, up_w)
            grad_units = mm_t(grad, down_w)
            activated, grad_gate, grad_up = gated(gate, up, grad_units)
            totals[0] += t_mm(normed, grad_gate)
            totals[1] += t_mm(normed, grad_up)
            totals[2] += t_mm(activated, grad)
        return [total.astype(bf16) for total in totals]

    both = tokens_whole(jnp.stack([hidden_in, out_grad]))
    resid = both[0].astype(f32)
    grad_start = both[1]
    own = resid.shape[0]

    saved = []
    earlier = None
    for layer in range(LAYERS):
        qkv_full, out_full = fetch_attention(layer, earlier)
        gate_w, up_w = fetch_wide(layer, earlier)
        down_w = fetch_narrow(layer, earlier)
        normed_attn, scale_attn = norm_forward(resid, attn_gain_full[layer])
        pair_attn = jnp.concatenate([normed_attn, swap_core(normed_attn)], axis=0)
        qkv_rows = mm(pair_attn, qkv_full) + bias_here[layer][None, :]
        attended, kept = attention_forward(qkv_rows, frame)
        out_part = mm(attended, out_full)
        out_other = swap_core(out_part[own:].astype(bf16))
        middle = resid + out_part[:own] + out_other.astype(f32)
        normed_mlp, scale_mlp = norm_forward(middle, mlp_gain_full[layer])
        all_mlp = gather_eight(normed_mlp)
        gate = mm(all_mlp, gate_w)
        up = mm(all_mlp, up_w)
        activated = (jax.nn.silu(gate) * up).astype(bf16)
        saved.append(
            (resid, scale_attn, pair_attn, kept, attended, middle, scale_mlp, all_mlp, gate, up,
             all_tokens(all_mlp), qkv_full, out_full, gate_w, up_w, down_w)
        )
        resid = middle + scatter_eight(mm(activated, down_w))
        earlier = all_mlp
    hidden_out = features_back(resid.astype(bf16))

    grad_resid = grad_start.astype(f32)
    grads = [None] * LAYERS
    small = [None] * LAYERS
    wide_out, narrow_out = None, None
    wide_parts, narrow_parts = [None] * LAYERS, [None] * LAYERS
    for layer in reversed(range(LAYERS)):
        (resid, scale_attn, pair_attn, kept, attended, middle, scale_mlp, all_mlp, gate, up,
         all_inputs, qkv_full, out_full, gate_w, up_w, down_w) = saved[layer]
        all_grad = gather_eight(grad_resid.astype(bf16))
        grad_units = mm_t(all_grad, down_w)
        _, grad_gate, grad_up = gated(gate, up, grad_units)
        grad_normed = scatter_eight(mm_t(grad_gate, gate_w) + mm_t(grad_up, up_w))
        gate_grad, up_grad, down_grad = mlp_weight_grads(
            all_inputs, all_tokens(all_grad), gate_w, up_w, down_w
        )
        if everyone:
            wide_out = give_wide((gate_grad, up_grad), layer, wide_out)
            narrow_out = give_narrow(down_grad, layer, narrow_out)
        else:
            wide_parts[layer] = (return_wide(gate_grad), return_wide(up_grad))
            narrow_parts[layer] = return_narrow(down_grad)
        grad_inner, mlp_gain_part = norm_backward(
            grad_normed, middle, scale_mlp, mlp_gain_full[layer]
        )
        grad_middle = grad_resid + grad_inner
        middle_round = grad_middle.astype(bf16)
        pair_grad = jnp.concatenate([middle_round, swap_core(middle_round)], axis=0)
        grad_heads = mm_t(pair_grad, out_full)
        out_grad_w = return_out(t_mm(attended, pair_grad))
        grad_qkv = attention_backward(grad_heads, kept, frame)
        bias_part = jnp.sum(grad_qkv, axis=0)
        qkv_round = grad_qkv.astype(bf16)
        grad_part = mm_t(qkv_round, qkv_full)
        grad_other = swap_core(grad_part[own:].astype(bf16))
        grad_normed_attn = grad_part[:own] + grad_other.astype(f32)
        qkv_grad_w = return_qkv(t_mm(pair_attn, qkv_round))
        grad_first, attn_gain_part = norm_backward(
            grad_normed_attn, resid, scale_attn, attn_gain_full[layer]
        )
        grad_resid = grad_middle + grad_first
        grads[layer] = (qkv_grad_w, out_grad_w)
        small[layer] = (attn_gain_part, mlp_gain_part, bias_part)
    in_grad = features_back(grad_resid.astype(bf16)).astype(f32)

    stacked = [
        jnp.stack([grads[layer][member].astype(f32) for layer in range(LAYERS)])
        for member in range(2)
    ]
    if everyone:
        stacked += [wide_out[0], wide_out[1], narrow_out[0]]
    else:
        stacked += [
            jnp.stack([wide_parts[layer][member].astype(f32) for layer in range(LAYERS)])
            for member in range(2)
        ]
        stacked.append(jnp.stack([narrow_parts[layer].astype(f32) for layer in range(LAYERS)]))
    bias_stack = jnp.stack([small[layer][2] for layer in range(LAYERS)])
    bias_full = jnp.where(
        core == 0,
        jnp.concatenate([bias_stack, jnp.zeros_like(bias_stack)], axis=1),
        jnp.concatenate([jnp.zeros_like(bias_stack), bias_stack], axis=1),
    )
    packed = jnp.concatenate(
        [
            jnp.stack([small[layer][0] for layer in range(LAYERS)]),
            jnp.stack([small[layer][1] for layer in range(LAYERS)]),
            bias_full,
        ],
        axis=1,
    )
    packed = packed + swap_core(packed)
    packed = packed + swap_x(packed)
    packed = packed + swap_y(packed)
    packed = jnp.sum(lax.all_gather(packed, DP, axis=0), axis=0)
    row_width = attn_gain.shape[1]
    col_width = b_qkv.shape[1]
    row_place = place * row_width
    attn_gain_grad = lax.dynamic_slice_in_dim(packed[:, :D], row_place, row_width, 1)
    mlp_gain_grad = lax.dynamic_slice_in_dim(packed[:, D : 2 * D], row_place, row_width, 1)
    bias_grad = lax.dynamic_slice_in_dim(packed[:, 2 * D :], column * col_width, col_width, 1)
    return (
        hidden_out,
        in_grad,
        attn_gain_grad,
        stacked[0],
        bias_grad,
        stacked[1],
        mlp_gain_grad,
        stacked[2],
        stacked[3],
        stacked[4],
    )


def solution(mesh):
    fine = Mesh(
        mesh.devices.reshape(mesh.shape["dp"], 2, mesh.shape["rows"] // 2, mesh.shape["cols"]),
        (DP, RY, RK, CX),
    )
    in_specs = (
        P((DP, CX), ROWS),
        P(None, ROWS),
        P(None, ROWS, CX),
        P(None, CX),
        P(None, CX, ROWS),
        P(None, ROWS),
        P(None, ROWS, CX),
        P(None, ROWS, CX),
        P(None, CX, ROWS),
        P((DP, CX), ROWS),
    )
    out_specs = (
        P((DP, CX), ROWS),
        P((DP, CX), ROWS),
        P(None, ROWS),
        P(None, ROWS, CX),
        P(None, CX),
        P(None, CX, ROWS),
        P(None, ROWS),
        P(None, ROWS, CX),
        P(None, ROWS, CX),
        P(None, CX, ROWS),
    )
    return jax.shard_map(body, mesh=fine, in_specs=in_specs, out_specs=out_specs, check_vma=False)
```

```python
import jax
import jax.numpy as jnp
import numpy as np
from jax import lax
from jax.experimental import pallas as pl
from jax.experimental.pallas import tpu as pltpu
from jax.sharding import Mesh, PartitionSpec as P


D = 1536
HEADS = 12
KV_HEADS = 2
HEAD_DIM = 128
SEQ = 192
LAYERS = 2
GROUP = HEADS // KV_HEADS

eps = 1e-06
theta = 1000000.0
masked = -1e30


DP, RY, RK, CX = "dp", "ry", "rk", "cols"
ROWS = (RY, RK)
PLANE = (RY, CX)

f32 = jnp.float32
bf16 = jnp.bfloat16


def mm(left, right):
    return jnp.dot(left, right, preferred_element_type=f32)


def mm_t(left, right):
    return lax.dot_general(left, right, (((1,), (1,)), ((), ())), preferred_element_type=f32)


def t_mm(left, right):
    return lax.dot_general(left, right, (((0,), (0,)), ((), ())), preferred_element_type=f32)


def swap_core(values):
    return lax.ppermute(values, RK, [(0, 1), (1, 0)])


def swap_x(values):
    return lax.ppermute(values, CX, [(0, 1), (1, 0)])


def swap_y(values):
    return lax.ppermute(values, RY, [(0, 1), (1, 0)])


def swap_diagonal(values):
    return lax.ppermute(values, (RK, CX), [(0, 0), (1, 2), (2, 1), (3, 3)])


def gather_eight(values):
    half = values.shape[0] // 2
    by_x = swap_x(values)
    by_y = swap_y(values)
    first = swap_x(by_y[:half])
    second = swap_y(by_x[half:])
    near = jnp.concatenate([values, by_x, by_y, first, second], axis=0)
    return jnp.concatenate([near, swap_core(near)], axis=0)


def scatter_eight(partial):
    rows = partial.shape[0] // 8
    half = rows // 2
    other = swap_core(partial[4 * rows :].astype(bf16))
    summed = partial[: 4 * rows] + other.astype(f32)
    own, to_x, to_y, corner = (summed[i * rows : (i + 1) * rows] for i in range(4))
    corner = corner.astype(bf16)
    via_x = swap_x(corner[:half]).astype(f32)
    via_y = swap_y(corner[half:]).astype(f32)
    to_y = jnp.concatenate([to_y[:half] + via_x, to_y[half:]], axis=0).astype(bf16)
    to_x = jnp.concatenate([to_x[:half], to_x[half:] + via_y], axis=0).astype(bf16)
    from_x = swap_x(to_x).astype(f32)
    return own + from_x + swap_y(to_y).astype(f32)


def rope_tables():
    frequency = theta ** (-np.arange(0, HEAD_DIM, 2, dtype=np.float32) / np.float32(HEAD_DIM))
    angles = np.arange(SEQ, dtype=np.float32)[:, None] * frequency[None, :].astype(np.float32)
    angles = np.concatenate([angles, angles], axis=-1).astype(np.float32)
    return np.cos(angles).astype(np.float32), np.sin(angles).astype(np.float32)


def rotate_half(values):
    half_dim = values.shape[-1] // 2
    return jnp.concatenate([-values[..., half_dim:], values[..., :half_dim]], axis=-1)


def attention_frame():
    second = lax.axis_index(RK) == 1
    cosine, sine = rope_tables()
    half = SEQ // 2
    cosine = jnp.where(second, np.roll(cosine, -half, axis=0), cosine)
    sine = jnp.where(second, np.roll(sine, -half, axis=0), sine)
    position = (jnp.arange(SEQ) + half * lax.axis_index(RK)) % SEQ
    mask = position[:, None] >= position[None, :]
    return cosine, sine, mask


def causal_scores(query_round, key_round, mask):
    raw_scores = jnp.einsum("igd,jd->gij", query_round, key_round, preferred_element_type=f32)
    return jnp.where(mask[None], raw_scores * HEAD_DIM ** (-0.5), masked)


def attention_forward(qkv_rows, frame):
    cosine, sine, mask = frame
    blocks = qkv_rows.reshape(SEQ, GROUP + 2, HEAD_DIM)
    turned = blocks[:, : GROUP + 1]
    turned = turned * cosine[:, None, :] + rotate_half(turned) * sine[:, None, :]
    turned = turned.astype(bf16)
    query_round = turned[:, :GROUP]
    key_round = turned[:, GROUP]
    value_round = blocks[:, GROUP + 1].astype(bf16)
    scores = causal_scores(query_round, key_round, mask)
    highest = jnp.max(scores, axis=-1, keepdims=True)
    log_total = highest + jnp.log(jnp.sum(jnp.exp(scores - highest), axis=-1, keepdims=True))
    weights_round = jnp.exp(scores - log_total).astype(bf16)
    attended = jnp.einsum("gij,jd->igd", weights_round, value_round, preferred_element_type=f32)
    attended = attended.astype(bf16).reshape(SEQ, -1)
    return attended, (query_round, key_round, value_round, log_total)


def attention_backward(grad_attended, kept, frame):
    cosine, sine, mask = frame
    query_round, key_round, value_round, log_total = kept
    grad_round = grad_attended.astype(bf16).reshape(SEQ, GROUP, HEAD_DIM)
    scores = causal_scores(query_round, key_round, mask)
    prob = jnp.exp(scores - log_total)
    weights_round = prob.astype(bf16)
    grad_value = jnp.einsum("gij,igd->jd", weights_round, grad_round, preferred_element_type=f32)
    grad_prob = jnp.einsum("igd,jd->gij", grad_round, value_round, preferred_element_type=f32)
    inner = jnp.sum(prob * grad_prob, axis=-1, keepdims=True)
    grad_scores = (prob * (grad_prob - inner) * HEAD_DIM ** (-0.5)).astype(bf16)
    grad_query = jnp.einsum("gij,jd->igd", grad_scores, key_round, preferred_element_type=f32)
    grad_key = jnp.einsum("gij,igd->jd", grad_scores, query_round, preferred_element_type=f32)
    turned = jnp.concatenate([grad_query, grad_key[:, None]], axis=1)
    turned = turned * cosine[:, None, :] - rotate_half(turned) * sine[:, None, :]
    joined = jnp.concatenate([turned, grad_value[:, None]], axis=1)
    return joined.reshape(SEQ, -1)


def norm_forward(resid, gain_row):
    scale_row = lax.rsqrt(jnp.mean(resid * resid, axis=1) + eps)
    normed = (resid * scale_row[:, None] * gain_row[None, :]).astype(bf16)
    return normed, scale_row


def norm_backward(grad_normed, resid, scale_row, gain_row):
    scaled = grad_normed * gain_row[None, :]
    inner = jnp.sum(scaled * resid, axis=1)
    gain_grad = jnp.sum(grad_normed * resid * scale_row[:, None], axis=0)
    grad_resid = (
        scale_row[:, None] * scaled
        - resid * (scale_row * scale_row * scale_row * inner / D)[:, None]
    )
    return grad_resid, gain_grad


def sum_dp(values):
    if lax.axis_size(DP) != 4:
        summed = lax.psum_scatter(values, DP, scatter_dimension=0, tiled=True)
        return lax.all_gather(summed, DP, axis=0, tiled=True)
    place = lax.axis_index(DP)
    inner = (place == 1) | (place == 2)
    kind = values.dtype
    inward = lax.ppermute(values, DP, [(0, 1), (3, 2)])
    half = (values.astype(f32) + inward.astype(f32)).astype(kind)
    across = lax.ppermute(half, DP, [(1, 2), (2, 1)])
    whole = (half.astype(f32) + across.astype(f32)).astype(kind)
    outward = lax.ppermute(whole, DP, [(1, 0), (2, 3)])
    return jnp.where(inner, whole, outward)


def gather_line(values):
    at = lax.axis_index(DP)
    inner = (at == 1) | (at == 2)
    pair = lax.ppermute(values, DP, [(0, 1), (1, 0), (2, 3), (3, 2)])
    middle = lax.ppermute(values, DP, [(1, 2), (2, 1)])
    outward = lax.ppermute(middle, DP, [(1, 0), (2, 3)])
    across = lax.ppermute(pair, DP, [(1, 2), (2, 1)])
    last = lax.ppermute(across, DP, [(1, 0), (2, 3)])
    third = jnp.where(inner, middle, outward)
    fourth = jnp.where(inner, across, last)
    blocks = [
        jnp.where(at == 0, values, jnp.where(at == 1, pair, fourth)),
        jnp.where(at == 1, values, jnp.where(at == 0, pair, third)),
        jnp.where(at == 2, values, jnp.where(at == 3, pair, third)),
        jnp.where(at == 3, values, jnp.where(at == 2, pair, fourth)),
    ]
    return jnp.concatenate(blocks, axis=0)


def xor_permute(values, bits):
    return lax.ppermute(values, ROWS, [(i, i ^ bits) for i in range(4)])


def swap_group(values):
    count = lax.axis_size(DP)
    return lax.ppermute(values, DP, [(i, i ^ 1) for i in range(count)])


PIECES = [(0, 1), (2, 2), (3, 3)]


def clamped(step, low, high):
    return jnp.clip(step - low, 0, high - low)


def take(arrays, table, layer, block, place, bound_dim, bound):
    count = len(arrays)
    rows, width = block

    def kernel(table_ref, *refs):
        step = pl.program_id(0)
        outs = refs[count:]
        for (low, high), out_ref in zip(PIECES, outs):

            @pl.when((step >= low) & (step <= high))
            def _():
                for i in range(count):
                    values = refs[i][...].reshape(rows, width)
                    if bound is not None:
                        first = place(2 + step, table_ref)[bound_dim] * block[bound_dim]
                        index = lax.broadcasted_iota(jnp.int32, (rows, width), bound_dim) + first
                        values = jnp.where(index < bound, values, jnp.zeros_like(values))
                    out_ref[i] = values

    if layer is None:
        in_spec = pl.BlockSpec(block, lambda i, s: place(2 + i, s))
    else:
        in_spec = pl.BlockSpec((1, *block), lambda i, s: (layer, *place(2 + i, s)))
    kind = arrays[0].dtype
    return pl.pallas_call(
        kernel,
        grid_spec=pltpu.PrefetchScalarGridSpec(
            num_scalar_prefetch=1,
            grid=(4,),
            in_specs=[in_spec] * count,
            out_specs=[
                pl.BlockSpec(
                    (count, rows, width), lambda i, s, low=low, high=high: (0, clamped(i, low, high), 0)
                )
                for low, high in PIECES
            ],
        ),
        out_shape=[
            jax.ShapeDtypeStruct((count, (high - low + 1) * rows, width), kind)
            for low, high in PIECES
        ],
    )(table, *arrays)


def join(arrays, parts, table, take_layer, block, take_place, bound_dim, bound, put_place, out_shape,
         dtype, layer=None, into=None):
    count = len(arrays)
    rows, width = block
    ranges = [(2, 3), (4, 4), (5, 5), (6, 6), (7, 7)]

    def kernel(table_ref, *refs):
        outs = refs[len(refs) - count :]
        piece = pl.program_id(0)

        @pl.when(piece <= 1)
        def _():
            for i in range(count):
                values = refs[i][...].reshape(rows, width)
                if bound is not None:
                    first = take_place(piece, table_ref)[bound_dim] * block[bound_dim]
                    index = lax.broadcasted_iota(jnp.int32, (rows, width), bound_dim) + first
                    values = jnp.where(index < bound, values, jnp.zeros_like(values))
                outs[i][...] = values.astype(dtype).reshape(outs[i].shape)

        for which, (low, high) in enumerate(ranges):

            @pl.when((piece >= low) & (piece <= high))
            def _():
                for i in range(count):
                    values = refs[count + which][i]
                    outs[i][...] = values.astype(dtype).reshape(outs[i].shape)

    if take_layer is None:
        own_spec = pl.BlockSpec(block, lambda i, s: take_place(jnp.minimum(i, 1), s))
    else:
        own_spec = pl.BlockSpec(
            (1, *block), lambda i, s: (take_layer, *take_place(jnp.minimum(i, 1), s))
        )
    in_specs = [own_spec] * count + [
        pl.BlockSpec(
            (count, rows, width), lambda i, s, low=low, high=high: (0, clamped(i, low, high), 0)
        )
        for low, high in ranges
    ]
    operands = [*arrays, *parts]
    aliases = {}
    if into is not None:
        for i, buffer in enumerate(into):
            aliases[1 + len(operands)] = i
            operands.append(buffer)
            in_specs.append(pl.BlockSpec(memory_space=pl.ANY))
    if layer is None:
        out_spec = pl.BlockSpec(block, lambda i, s: put_place(i, s))
    else:
        out_spec = pl.BlockSpec((1, *block), lambda i, s: (layer, *put_place(i, s)))
    return pl.pallas_call(
        kernel,
        grid_spec=pltpu.PrefetchScalarGridSpec(
            num_scalar_prefetch=1,
            grid=(8,),
            in_specs=in_specs,
            out_specs=[out_spec] * count,
        ),
        out_shape=[jax.ShapeDtypeStruct(out_shape, dtype)] * count,
        input_output_aliases=aliases,
    )(table, *operands)


def gated_all(normed, grads, gate_w, up_w, down_w):
    half, share = normed[0].shape[0], gate_w.shape[1]
    rows, width = 512, share // 3
    steps = half // rows

    def kernel(xn_ref, xf_ref, gn_ref, gf_ref, gate_ref, up_ref, down_ref, *outs):
        x_ref, g_ref, act_ref, dgate_ref, dup_ref = outs
        step = pl.program_id(0)

        @pl.when(step < steps)
        def _():
            x_ref[...] = xn_ref[...]
            g_ref[...] = gn_ref[...]

        @pl.when(step >= steps)
        def _():
            x_ref[...] = xf_ref[...]
            g_ref[...] = gf_ref[...]

        for tile in range(3):
            part = slice(tile * width, (tile + 1) * width)
            gate = mm(x_ref[...], gate_ref[:, part])
            up = mm(x_ref[...], up_ref[:, part])
            grad_units = mm_t(g_ref[...], down_ref[part, :])
            act_ref[:, part], dgate_ref[:, part], dup_ref[:, part] = gated(gate, up, grad_units)

    near_spec = pl.BlockSpec((rows, D), lambda i: (jnp.minimum(i, steps - 1), 0))
    far_spec = pl.BlockSpec((rows, D), lambda i: (jnp.maximum(i - steps, 0), 0))
    token_spec = pl.BlockSpec((rows, D), lambda i: (i, 0))
    out_spec = pl.BlockSpec((rows, share), lambda i: (i, 0))
    whole = [pl.BlockSpec(weight.shape, lambda i: (0, 0)) for weight in (gate_w, up_w, down_w)]
    tokens = 2 * half
    return pl.pallas_call(
        kernel,
        grid=(2 * steps,),
        in_specs=[near_spec, far_spec, near_spec, far_spec, *whole],
        out_specs=[token_spec] * 2 + [out_spec] * 3,
        out_shape=[jax.ShapeDtypeStruct((tokens, D), bf16)] * 2
        + [jax.ShapeDtypeStruct((tokens, share), bf16)] * 3,
        cost_estimate=pl.CostEstimate(
            flops=6 * tokens * share * D,
            bytes_accessed=2 * (4 * tokens * D + 3 * share * D + 3 * tokens * share),
            transcendentals=tokens * share,
        ),
    )(*normed, *grads, gate_w, up_w, down_w)


def gated(gate, up, grad_units):
    sigmoid_gate = jax.nn.sigmoid(gate)
    activated = (gate * sigmoid_gate * up).astype(bf16)
    grad_gate = grad_units * up * sigmoid_gate * (1.0 + gate * (1.0 - sigmoid_gate))
    grad_up = grad_units * gate * sigmoid_gate
    return activated, grad_gate.astype(bf16), grad_up.astype(bf16)


def body(hidden_in, attn_gain, w_qkv, b_qkv, w_out, mlp_gain, w_gate, w_up, w_down, out_grad):
    units = w_gate.shape[2]
    share = -(-units // (4 * 128)) * 128
    core = lax.axis_index(RK)
    column = lax.axis_index(CX)
    frame = attention_frame()
    everyone = lax.axis_size(DP) == 4

    place = lax.axis_index(RY) * 2 + core
    gains = lax.dynamic_update_slice(
        jnp.zeros((2 * LAYERS, D), f32),
        jnp.concatenate([attn_gain, mlp_gain], axis=0),
        (0, place * attn_gain.shape[1]),
    )
    gains = gains + swap_core(gains)
    gains = gains + swap_y(gains)
    attn_gain_full, mlp_gain_full = gains[:LAYERS], gains[LAYERS:]
    bias_other = swap_x(b_qkv)
    bias_here = jnp.where(core == column, b_qkv, bias_other)

    def tokens_whole(values):
        count, rows, width = values.shape
        blocks = values.reshape(count, 4, rows // 4, width)
        parts = []
        for bits in range(4):
            part = lax.dynamic_index_in_dim(blocks, place ^ bits, 1, keepdims=False)
            parts.append(part if bits == 0 else xor_permute(part, bits))
        parts = [jnp.where(core == 1, parts[i ^ 1], parts[i]) for i in range(4)]
        parts = [jnp.where(place >= 2, parts[i ^ 2], parts[i]) for i in range(4)]
        return jnp.concatenate(parts, axis=-1)

    def features_back(values):
        rows, width = values.shape[0], values.shape[1] // 4
        blocks = jnp.stack([values[:, i * width : (i + 1) * width] for i in range(4)])
        return lax.all_to_all(blocks, ROWS, 0, 0, tiled=True).reshape(4 * rows, width)

    def fetch_attention(layer):
        qkv_near = swap_diagonal(w_qkv[layer])
        out_near = swap_diagonal(w_out[layer])
        qkv_block = lax.all_gather(qkv_near, PLANE, axis=0)
        out_block = lax.all_gather(out_near, PLANE, axis=0)
        qkv_full = qkv_block.reshape(D, -1)
        out_full = jnp.concatenate([out_block[i] for i in range(4)], axis=1)
        return qkv_full, out_full

    half_d = D // 8
    unit_half = share // 2
    parity = lax.axis_index(DP) % 2
    sources = [place ^ bits for bits in range(4)]
    zero, one = jnp.int32(0), jnp.int32(1)
    take_table = jnp.stack(
        [sources[0], sources[0], sources[1], sources[1], sources[2], sources[3]]
        + [zero, one, zero, one, parity, parity]
    ).astype(jnp.int32)
    put_table = jnp.stack(
        [sources[i // 2] for i in range(8)] + [zero, one] * 2 + [parity, 1 - parity] * 2
    ).astype(jnp.int32)
    table = jnp.concatenate([take_table, put_table])

    def block_of(i, s):
        return s[i]

    def half_of(i, s):
        return s[6 + i]

    def put_block(i, s):
        return s[12 + i]

    def put_half(i, s):
        return s[20 + i]

    def exchange(sent):
        core_part, y_part, corner_part = sent
        y_mine = xor_permute(y_part, 2)
        corner_mine = xor_permute(corner_part, 3)
        return (
            swap_core(core_part), y_mine, swap_group(y_mine), corner_mine, swap_group(corner_mine)
        )

    def moved(arrays, from_layer, block, source, bound_dim, bound, target, shape, dtype,
              layer=None, into=None):
        sent = take(arrays, table, from_layer, block, source, bound_dim, bound)
        parts = exchange(sent)
        return join(
            arrays, parts, table, from_layer, block, source, bound_dim, bound, target, shape,
            dtype, layer, into,
        )

    def fetch_wide(layer):
        return moved(
            (w_gate, w_up), layer, (half_d, share),
            lambda i, s: (half_of(i, s), block_of(i, s)), 1, units,
            lambda i, s: (2 * put_block(i, s) + put_half(i, s), 0), (D, share), bf16,
        )

    def fetch_narrow(layer):
        return moved(
            (w_down,), layer, (unit_half, D // 4),
            lambda i, s: (2 * block_of(i, s) + half_of(i, s), 0), 0, units,
            lambda i, s: (put_half(i, s), put_block(i, s)), (share, D), bf16,
        )[0]

    def give_wide(grad, layer, into):
        return moved(
            (grad,), None, (half_d, share),
            lambda i, s: (2 * block_of(i, s) + half_of(i, s), 0), 0, None,
            lambda i, s: (put_half(i, s), put_block(i, s)), w_gate.shape, f32, layer, into,
        )

    def give_narrow(grad, layer, into):
        return moved(
            (grad,), None, (unit_half, D // 4),
            lambda i, s: (half_of(i, s), block_of(i, s)), 0, None,
            lambda i, s: (2 * put_block(i, s) + put_half(i, s), 0), w_down.shape, f32, layer, into,
        )

    def return_wide(grad):
        blocks = grad.astype(bf16).reshape(4, D // 4, share)
        arrived = lax.all_to_all(blocks, ROWS, 0, 0, tiled=True)
        spread = jnp.concatenate([arrived[i] for i in range(4)], axis=1)[:, :units]
        return sum_dp(spread)

    def return_narrow(grad):
        rows = grad.astype(bf16)
        blocks = jnp.stack([rows[:, i * (D // 4) : (i + 1) * (D // 4)] for i in range(4)])
        arrived = lax.all_to_all(blocks, ROWS, 0, 0, tiled=True)
        spread = arrived.reshape(4 * share, -1)[:units]
        return sum_dp(spread)

    def return_qkv(grad):
        blocks = grad.astype(bf16).reshape(4, D // 4, -1)
        summed = lax.psum_scatter(blocks, PLANE)
        return sum_dp(swap_diagonal(summed))

    def return_out(grad):
        rows = grad.astype(bf16)
        blocks = jnp.stack([rows[:, i * (D // 4) : (i + 1) * (D // 4)] for i in range(4)])
        summed = lax.psum_scatter(blocks, PLANE)
        return sum_dp(swap_diagonal(summed))

    def all_tokens(values, by_line):
        mine = values[: values.shape[0] // 2]
        if by_line:
            near = gather_line(mine)
        else:
            near = lax.all_gather(mine, DP, axis=0, tiled=True)
        return near, swap_core(near)

    def mlp_weight_grads(normed, grads, gate_w, up_w, down_w):
        normed, grads, activated, grad_gate, grad_up = gated_all(
            normed, grads, gate_w, up_w, down_w
        )
        return (
            t_mm(normed, grad_gate).astype(bf16),
            t_mm(normed, grad_up).astype(bf16),
            t_mm(activated, grads).astype(bf16),
        )

    both = tokens_whole(jnp.stack([hidden_in, out_grad]))
    resid = both[0].astype(f32)
    grad_start = both[1]
    own = resid.shape[0]

    saved = []
    for layer in range(LAYERS):
        qkv_full, out_full = fetch_attention(layer)
        gate_w, up_w = fetch_wide(layer)
        down_w = fetch_narrow(layer)
        normed_attn, scale_attn = norm_forward(resid, attn_gain_full[layer])
        pair_attn = jnp.concatenate([normed_attn, swap_core(normed_attn)], axis=0)
        qkv_rows = mm(pair_attn, qkv_full) + bias_here[layer][None, :]
        attended, kept = attention_forward(qkv_rows, frame)
        out_part = mm(attended, out_full)
        out_other = swap_core(out_part[own:].astype(bf16))
        middle = resid + out_part[:own] + out_other.astype(f32)
        normed_mlp, scale_mlp = norm_forward(middle, mlp_gain_full[layer])
        all_mlp = gather_eight(normed_mlp)
        gate = mm(all_mlp, gate_w)
        up = mm(all_mlp, up_w)
        activated = (jax.nn.silu(gate) * up).astype(bf16)
        saved.append(
            (resid, scale_attn, pair_attn, kept, attended, middle, scale_mlp, all_mlp, gate, up,
             activated, qkv_full, out_full, gate_w, up_w, down_w)
        )
        if layer < LAYERS - 1:
            resid = middle + scatter_eight(mm(activated, down_w))

    grad_resid = grad_start.astype(f32)
    grads = [None] * LAYERS
    small = [None] * LAYERS
    gate_out, up_out, narrow_out = None, None, None
    wide_parts, narrow_parts = [None] * LAYERS, [None] * LAYERS
    for layer in reversed(range(LAYERS)):
        (resid, scale_attn, pair_attn, kept, attended, middle, scale_mlp, all_mlp, gate, up,
         activated, qkv_full, out_full, gate_w, up_w, down_w) = saved[layer]
        all_grad = gather_eight(grad_resid.astype(bf16))
        if layer == 0:
            late = saved[LAYERS - 1]
            late_middle, late_units, _ = lax.optimization_barrier((late[5], late[10], all_grad))
            last_part = mm(late_units, late[15])
            resid_out = late_middle + scatter_eight(last_part)
            hidden_out = features_back(resid_out.astype(bf16))
        grad_units = mm_t(all_grad, down_w)
        _, grad_gate, grad_up = gated(gate, up, grad_units)
        grad_normed = scatter_eight(mm_t(grad_gate, gate_w) + mm_t(grad_up, up_w))
        if everyone:
            gate_grad, up_grad, down_grad = mlp_weight_grads(
                all_tokens(all_mlp, layer == LAYERS - 1),
                all_tokens(all_grad, layer < LAYERS - 1),
                gate_w, up_w, down_w,
            )
            narrow_out = give_narrow(down_grad, layer, narrow_out)
            gate_out = give_wide(gate_grad, layer, gate_out)
            up_out = give_wide(up_grad, layer, up_out)
        else:
            wide_parts[layer] = (
                return_wide(t_mm(all_mlp, grad_gate)),
                return_wide(t_mm(all_mlp, grad_up)),
            )
            narrow_parts[layer] = return_narrow(t_mm(activated, all_grad))
        grad_inner, mlp_gain_part = norm_backward(
            grad_normed, middle, scale_mlp, mlp_gain_full[layer]
        )
        grad_middle = grad_resid + grad_inner
        middle_round = grad_middle.astype(bf16)
        pair_grad = jnp.concatenate([middle_round, swap_core(middle_round)], axis=0)
        grad_heads = mm_t(pair_grad, out_full)
        out_grad_w = return_out(t_mm(attended, pair_grad))
        grad_qkv = attention_backward(grad_heads, kept, frame)
        bias_part = jnp.sum(grad_qkv, axis=0)
        qkv_round = grad_qkv.astype(bf16)
        grad_part = mm_t(qkv_round, qkv_full)
        grad_other = swap_core(grad_part[own:].astype(bf16))
        grad_normed_attn = grad_part[:own] + grad_other.astype(f32)
        qkv_grad_w = return_qkv(t_mm(pair_attn, qkv_round))
        grad_first, attn_gain_part = norm_backward(
            grad_normed_attn, resid, scale_attn, attn_gain_full[layer]
        )
        grad_resid = grad_middle + grad_first
        grads[layer] = (qkv_grad_w, out_grad_w)
        small[layer] = (attn_gain_part, mlp_gain_part, bias_part)
    in_grad = features_back(grad_resid.astype(bf16)).astype(f32)

    stacked = [
        jnp.stack([grads[layer][member].astype(f32) for layer in range(LAYERS)])
        for member in range(2)
    ]
    if everyone:
        stacked += [gate_out[0], up_out[0], narrow_out[0]]
    else:
        stacked += [
            jnp.stack([wide_parts[layer][member].astype(f32) for layer in range(LAYERS)])
            for member in range(2)
        ]
        stacked.append(jnp.stack([narrow_parts[layer].astype(f32) for layer in range(LAYERS)]))
    bias_stack = jnp.stack([small[layer][2] for layer in range(LAYERS)])
    bias_full = jnp.where(
        core == 0,
        jnp.concatenate([bias_stack, jnp.zeros_like(bias_stack)], axis=1),
        jnp.concatenate([jnp.zeros_like(bias_stack), bias_stack], axis=1),
    )
    packed = jnp.concatenate(
        [
            jnp.stack([small[layer][0] for layer in range(LAYERS)]),
            jnp.stack([small[layer][1] for layer in range(LAYERS)]),
            bias_full,
        ],
        axis=1,
    )
    packed = packed + swap_core(packed)
    packed = packed + swap_x(packed)
    packed = packed + swap_y(packed)
    if everyone:
        packed = sum_dp(packed)
    else:
        packed = lax.psum(packed, DP)
    row_width = attn_gain.shape[1]
    col_width = b_qkv.shape[1]
    row_place = place * row_width
    attn_gain_grad = lax.dynamic_slice_in_dim(packed[:, :D], row_place, row_width, 1)
    mlp_gain_grad = lax.dynamic_slice_in_dim(packed[:, D : 2 * D], row_place, row_width, 1)
    bias_grad = lax.dynamic_slice_in_dim(packed[:, 2 * D :], column * col_width, col_width, 1)
    return (
        hidden_out,
        in_grad,
        attn_gain_grad,
        stacked[0],
        bias_grad,
        stacked[1],
        mlp_gain_grad,
        stacked[2],
        stacked[3],
        stacked[4],
    )


def solution(mesh):
    fine = Mesh(
        mesh.devices.reshape(mesh.shape["dp"], 2, mesh.shape["rows"] // 2, mesh.shape["cols"]),
        (DP, RY, RK, CX),
    )
    in_specs = (
        P((DP, CX), ROWS),
        P(None, ROWS),
        P(None, ROWS, CX),
        P(None, CX),
        P(None, CX, ROWS),
        P(None, ROWS),
        P(None, ROWS, CX),
        P(None, ROWS, CX),
        P(None, CX, ROWS),
        P((DP, CX), ROWS),
    )
    out_specs = (
        P((DP, CX), ROWS),
        P((DP, CX), ROWS),
        P(None, ROWS),
        P(None, ROWS, CX),
        P(None, CX),
        P(None, CX, ROWS),
        P(None, ROWS),
        P(None, ROWS, CX),
        P(None, ROWS, CX),
        P(None, CX, ROWS),
    )

    return jax.shard_map(body, mesh=fine, in_specs=in_specs, out_specs=out_specs, check_vma=False)
```

```python
import jax
import jax.numpy as jnp
import numpy as np
from jax import lax
from jax.experimental import pallas as pl
from jax.experimental.pallas import tpu as pltpu
from jax.sharding import Mesh, PartitionSpec as P


D = 1536
HEADS = 12
KV_HEADS = 2
HEAD_DIM = 128
SEQ = 192
LAYERS = 2
GROUP = HEADS // KV_HEADS

eps = 1e-06
theta = 1000000.0
masked = -1e30


DP, RY, RK, CX = "dp", "ry", "rk", "cols"
ROWS = (RY, RK)
PLANE = (RY, CX)

f32 = jnp.float32
bf16 = jnp.bfloat16


def mm(left, right):
    return jnp.dot(left, right, preferred_element_type=f32)


def mm_t(left, right):
    return lax.dot_general(left, right, (((1,), (1,)), ((), ())), preferred_element_type=f32)


def t_mm(left, right):
    return lax.dot_general(left, right, (((0,), (0,)), ((), ())), preferred_element_type=f32)


def swap_core(values):
    return lax.ppermute(values, RK, [(0, 1), (1, 0)])


def swap_x(values):
    return lax.ppermute(values, CX, [(0, 1), (1, 0)])


def swap_y(values):
    return lax.ppermute(values, RY, [(0, 1), (1, 0)])


def swap_diagonal(values):
    return lax.ppermute(values, (RK, CX), [(0, 0), (1, 2), (2, 1), (3, 3)])


def gather_eight(values):
    half = values.shape[0] // 2
    by_x = swap_x(values)
    by_y = swap_y(values)
    first = swap_x(by_y[:half])
    second = swap_y(by_x[half:])
    near = jnp.concatenate([values, by_x, by_y, first, second], axis=0)
    return jnp.concatenate([near, swap_core(near)], axis=0)


def scatter_eight(partial):
    rows = partial.shape[0] // 8
    half = rows // 2
    other = swap_core(partial[4 * rows :].astype(bf16))
    summed = partial[: 4 * rows] + other.astype(f32)
    own, to_x, to_y, corner = (summed[i * rows : (i + 1) * rows] for i in range(4))
    corner = corner.astype(bf16)
    via_x = swap_x(corner[:half]).astype(f32)
    via_y = swap_y(corner[half:]).astype(f32)
    to_y = jnp.concatenate([to_y[:half] + via_x, to_y[half:]], axis=0).astype(bf16)
    to_x = jnp.concatenate([to_x[:half], to_x[half:] + via_y], axis=0).astype(bf16)
    from_x = swap_x(to_x).astype(f32)
    return own + from_x + swap_y(to_y).astype(f32)


def rope_tables():
    frequency = theta ** (-np.arange(0, HEAD_DIM, 2, dtype=np.float32) / np.float32(HEAD_DIM))
    angles = np.arange(SEQ, dtype=np.float32)[:, None] * frequency[None, :].astype(np.float32)
    angles = np.concatenate([angles, angles], axis=-1).astype(np.float32)
    return np.cos(angles).astype(np.float32), np.sin(angles).astype(np.float32)


def rotate_half(values):
    half_dim = values.shape[-1] // 2
    return jnp.concatenate([-values[..., half_dim:], values[..., :half_dim]], axis=-1)


def attention_frame():
    second = lax.axis_index(RK) == 1
    cosine, sine = rope_tables()
    half = SEQ // 2
    cosine = jnp.where(second, np.roll(cosine, -half, axis=0), cosine)
    sine = jnp.where(second, np.roll(sine, -half, axis=0), sine)
    position = (jnp.arange(SEQ) + half * lax.axis_index(RK)) % SEQ
    mask = position[:, None] >= position[None, :]
    return cosine, sine, mask


def causal_scores(query_round, key_round, mask):
    raw_scores = jnp.einsum("igd,jd->gij", query_round, key_round, preferred_element_type=f32)
    return jnp.where(mask[None], raw_scores * HEAD_DIM ** (-0.5), masked)


def attention_forward(qkv_rows, frame):
    cosine, sine, mask = frame
    blocks = qkv_rows.reshape(SEQ, GROUP + 2, HEAD_DIM)
    turned = blocks[:, : GROUP + 1]
    turned = turned * cosine[:, None, :] + rotate_half(turned) * sine[:, None, :]
    turned = turned.astype(bf16)
    query_round = turned[:, :GROUP]
    key_round = turned[:, GROUP]
    value_round = blocks[:, GROUP + 1].astype(bf16)
    scores = causal_scores(query_round, key_round, mask)
    highest = jnp.max(scores, axis=-1, keepdims=True)
    log_total = highest + jnp.log(jnp.sum(jnp.exp(scores - highest), axis=-1, keepdims=True))
    weights_round = jnp.exp(scores - log_total).astype(bf16)
    attended = jnp.einsum("gij,jd->igd", weights_round, value_round, preferred_element_type=f32)
    attended = attended.astype(bf16).reshape(SEQ, -1)
    return attended, (query_round, key_round, value_round, log_total)


def attention_backward(grad_attended, kept, frame):
    cosine, sine, mask = frame
    query_round, key_round, value_round, log_total = kept
    grad_round = grad_attended.astype(bf16).reshape(SEQ, GROUP, HEAD_DIM)
    scores = causal_scores(query_round, key_round, mask)
    prob = jnp.exp(scores - log_total)
    weights_round = prob.astype(bf16)
    grad_value = jnp.einsum("gij,igd->jd", weights_round, grad_round, preferred_element_type=f32)
    grad_prob = jnp.einsum("igd,jd->gij", grad_round, value_round, preferred_element_type=f32)
    inner = jnp.sum(prob * grad_prob, axis=-1, keepdims=True)
    grad_scores = (prob * (grad_prob - inner) * HEAD_DIM ** (-0.5)).astype(bf16)
    grad_query = jnp.einsum("gij,jd->igd", grad_scores, key_round, preferred_element_type=f32)
    grad_key = jnp.einsum("gij,igd->jd", grad_scores, query_round, preferred_element_type=f32)
    turned = jnp.concatenate([grad_query, grad_key[:, None]], axis=1)
    turned = turned * cosine[:, None, :] - rotate_half(turned) * sine[:, None, :]
    joined = jnp.concatenate([turned, grad_value[:, None]], axis=1)
    return joined.reshape(SEQ, -1)


def norm_forward(resid, gain_row):
    scale_row = lax.rsqrt(jnp.mean(resid * resid, axis=1) + eps)
    normed = (resid * scale_row[:, None] * gain_row[None, :]).astype(bf16)
    return normed, scale_row


def norm_backward(grad_normed, resid, scale_row, gain_row):
    scaled = grad_normed * gain_row[None, :]
    inner = jnp.sum(scaled * resid, axis=1)
    gain_grad = jnp.sum(grad_normed * resid * scale_row[:, None], axis=0)
    grad_resid = (
        scale_row[:, None] * scaled
        - resid * (scale_row * scale_row * scale_row * inner / D)[:, None]
    )
    return grad_resid, gain_grad


def sum_dp(values):
    if lax.axis_size(DP) != 4:
        summed = lax.psum_scatter(values, DP, scatter_dimension=0, tiled=True)
        return lax.all_gather(summed, DP, axis=0, tiled=True)
    place = lax.axis_index(DP)
    inner = (place == 1) | (place == 2)
    kind = values.dtype
    inward = lax.ppermute(values, DP, [(0, 1), (3, 2)])
    half = (values.astype(f32) + inward.astype(f32)).astype(kind)
    across = lax.ppermute(half, DP, [(1, 2), (2, 1)])
    whole = (half.astype(f32) + across.astype(f32)).astype(kind)
    outward = lax.ppermute(whole, DP, [(1, 0), (2, 3)])
    return jnp.where(inner, whole, outward)


def gather_line(values):
    at = lax.axis_index(DP)
    inner = (at == 1) | (at == 2)
    pair = lax.ppermute(values, DP, [(0, 1), (1, 0), (2, 3), (3, 2)])
    middle = lax.ppermute(values, DP, [(1, 2), (2, 1)])
    outward = lax.ppermute(middle, DP, [(1, 0), (2, 3)])
    across = lax.ppermute(pair, DP, [(1, 2), (2, 1)])
    last = lax.ppermute(across, DP, [(1, 0), (2, 3)])
    third = jnp.where(inner, middle, outward)
    fourth = jnp.where(inner, across, last)
    blocks = [
        jnp.where(at == 0, values, jnp.where(at == 1, pair, fourth)),
        jnp.where(at == 1, values, jnp.where(at == 0, pair, third)),
        jnp.where(at == 2, values, jnp.where(at == 3, pair, third)),
        jnp.where(at == 3, values, jnp.where(at == 2, pair, fourth)),
    ]
    return jnp.concatenate(blocks, axis=0)


def xor_permute(values, bits):
    return lax.ppermute(values, ROWS, [(i, i ^ bits) for i in range(4)])


def swap_group(values):
    count = lax.axis_size(DP)
    return lax.ppermute(values, DP, [(i, i ^ 1) for i in range(count)])


PIECES = [(0, 1), (2, 2), (3, 3)]


def clamped(step, low, high):
    return jnp.clip(step - low, 0, high - low)


def take(arrays, table, layer, block, place, bound_dim, bound):
    count = len(arrays)
    rows, width = block

    def kernel(table_ref, *refs):
        step = pl.program_id(0)
        outs = refs[count:]
        for (low, high), out_ref in zip(PIECES, outs):

            @pl.when((step >= low) & (step <= high))
            def _():
                for i in range(count):
                    values = refs[i][...].reshape(rows, width)
                    if bound is not None:
                        first = place(2 + step, table_ref)[bound_dim] * block[bound_dim]
                        index = lax.broadcasted_iota(jnp.int32, (rows, width), bound_dim) + first
                        values = jnp.where(index < bound, values, jnp.zeros_like(values))
                    out_ref[i] = values

    if layer is None:
        in_spec = pl.BlockSpec(block, lambda i, s: place(2 + i, s))
    else:
        in_spec = pl.BlockSpec((1, *block), lambda i, s: (layer, *place(2 + i, s)))
    kind = arrays[0].dtype
    return pl.pallas_call(
        kernel,
        grid_spec=pltpu.PrefetchScalarGridSpec(
            num_scalar_prefetch=1,
            grid=(4,),
            in_specs=[in_spec] * count,
            out_specs=[
                pl.BlockSpec(
                    (count, rows, width), lambda i, s, low=low, high=high: (0, clamped(i, low, high), 0)
                )
                for low, high in PIECES
            ],
        ),
        out_shape=[
            jax.ShapeDtypeStruct((count, (high - low + 1) * rows, width), kind)
            for low, high in PIECES
        ],
    )(table, *arrays)


def join(arrays, parts, table, take_layer, block, take_place, bound_dim, bound, put_place, out_shape,
         dtype, layer=None, into=None):
    count = len(arrays)
    rows, width = block
    ranges = [(2, 3), (4, 4), (5, 5), (6, 6), (7, 7)]

    def kernel(table_ref, *refs):
        outs = refs[len(refs) - count :]
        piece = pl.program_id(0)

        @pl.when(piece <= 1)
        def _():
            for i in range(count):
                values = refs[i][...].reshape(rows, width)
                if bound is not None:
                    first = take_place(piece, table_ref)[bound_dim] * block[bound_dim]
                    index = lax.broadcasted_iota(jnp.int32, (rows, width), bound_dim) + first
                    values = jnp.where(index < bound, values, jnp.zeros_like(values))
                outs[i][...] = values.astype(dtype).reshape(outs[i].shape)

        for which, (low, high) in enumerate(ranges):

            @pl.when((piece >= low) & (piece <= high))
            def _():
                for i in range(count):
                    values = refs[count + which][i]
                    outs[i][...] = values.astype(dtype).reshape(outs[i].shape)

    if take_layer is None:
        own_spec = pl.BlockSpec(block, lambda i, s: take_place(jnp.minimum(i, 1), s))
    else:
        own_spec = pl.BlockSpec(
            (1, *block), lambda i, s: (take_layer, *take_place(jnp.minimum(i, 1), s))
        )
    in_specs = [own_spec] * count + [
        pl.BlockSpec(
            (count, rows, width), lambda i, s, low=low, high=high: (0, clamped(i, low, high), 0)
        )
        for low, high in ranges
    ]
    operands = [*arrays, *parts]
    aliases = {}
    if into is not None:
        for i, buffer in enumerate(into):
            aliases[1 + len(operands)] = i
            operands.append(buffer)
            in_specs.append(pl.BlockSpec(memory_space=pl.ANY))
    if layer is None:
        out_spec = pl.BlockSpec(block, lambda i, s: put_place(i, s))
    else:
        out_spec = pl.BlockSpec((1, *block), lambda i, s: (layer, *put_place(i, s)))
    return pl.pallas_call(
        kernel,
        grid_spec=pltpu.PrefetchScalarGridSpec(
            num_scalar_prefetch=1,
            grid=(8,),
            in_specs=in_specs,
            out_specs=[out_spec] * count,
        ),
        out_shape=[jax.ShapeDtypeStruct(out_shape, dtype)] * count,
        input_output_aliases=aliases,
    )(table, *operands)


def gated_all(normed, grads, gate_w, up_w, down_w):
    half, share = normed[0].shape[0], gate_w.shape[1]
    rows, width = 512, share // 3
    steps = half // rows
    down_t = down_w.T

    def kernel(xn_ref, xf_ref, gn_ref, gf_ref, gate_ref, up_ref, down_ref, *outs):
        x_ref, g_ref, act_ref, dgate_ref, dup_ref = outs
        step = pl.program_id(0)

        @pl.when(step < steps)
        def _():
            x_ref[...] = xn_ref[...]
            g_ref[...] = gn_ref[...]

        @pl.when(step >= steps)
        def _():
            x_ref[...] = xf_ref[...]
            g_ref[...] = gf_ref[...]

        for tile in range(3):
            part = slice(tile * width, (tile + 1) * width)
            gate = mm(x_ref[...], gate_ref[:, part])
            up = mm(x_ref[...], up_ref[:, part])
            grad_units = mm(g_ref[...], down_ref[:, part])
            act_ref[:, part], dgate_ref[:, part], dup_ref[:, part] = gated(gate, up, grad_units)

    near_spec = pl.BlockSpec((rows, D), lambda i: (jnp.minimum(i, steps - 1), 0))
    far_spec = pl.BlockSpec((rows, D), lambda i: (jnp.maximum(i - steps, 0), 0))
    token_spec = pl.BlockSpec((rows, D), lambda i: (i, 0))
    out_spec = pl.BlockSpec((rows, share), lambda i: (i, 0))
    whole = [pl.BlockSpec(weight.shape, lambda i: (0, 0)) for weight in (gate_w, up_w, down_t)]
    tokens = 2 * half
    return pl.pallas_call(
        kernel,
        grid=(2 * steps,),
        in_specs=[near_spec, far_spec, near_spec, far_spec, *whole],
        out_specs=[token_spec] * 2 + [out_spec] * 3,
        out_shape=[jax.ShapeDtypeStruct((tokens, D), bf16)] * 2
        + [jax.ShapeDtypeStruct((tokens, share), bf16)] * 3,
        cost_estimate=pl.CostEstimate(
            flops=6 * tokens * share * D,
            bytes_accessed=2 * (4 * tokens * D + 3 * share * D + 3 * tokens * share),
            transcendentals=tokens * share,
        ),
    )(*normed, *grads, gate_w, up_w, down_t)


def gated(gate, up, grad_units):
    sigmoid_gate = jax.nn.sigmoid(gate)
    activated = (gate * sigmoid_gate * up).astype(bf16)
    grad_gate = grad_units * up * sigmoid_gate * (1.0 + gate * (1.0 - sigmoid_gate))
    grad_up = grad_units * gate * sigmoid_gate
    return activated, grad_gate.astype(bf16), grad_up.astype(bf16)


def body(hidden_in, attn_gain, w_qkv, b_qkv, w_out, mlp_gain, w_gate, w_up, w_down, out_grad):
    units = w_gate.shape[2]
    share = -(-units // (4 * 128)) * 128
    core = lax.axis_index(RK)
    column = lax.axis_index(CX)
    frame = attention_frame()
    everyone = lax.axis_size(DP) == 4

    place = lax.axis_index(RY) * 2 + core
    gains = lax.dynamic_update_slice(
        jnp.zeros((2 * LAYERS, D), f32),
        jnp.concatenate([attn_gain, mlp_gain], axis=0),
        (0, place * attn_gain.shape[1]),
    )
    gains = gains + swap_core(gains)
    gains = gains + swap_y(gains)
    attn_gain_full, mlp_gain_full = gains[:LAYERS], gains[LAYERS:]
    bias_other = swap_x(b_qkv)
    bias_here = jnp.where(core == column, b_qkv, bias_other)

    def tokens_whole(values):
        count, rows, width = values.shape
        blocks = values.reshape(count, 4, rows // 4, width)
        parts = []
        for bits in range(4):
            part = lax.dynamic_index_in_dim(blocks, place ^ bits, 1, keepdims=False)
            parts.append(part if bits == 0 else xor_permute(part, bits))
        parts = [jnp.where(core == 1, parts[i ^ 1], parts[i]) for i in range(4)]
        parts = [jnp.where(place >= 2, parts[i ^ 2], parts[i]) for i in range(4)]
        return jnp.concatenate(parts, axis=-1)

    def features_back(values):
        rows, width = values.shape[0], values.shape[1] // 4
        blocks = jnp.stack([values[:, i * width : (i + 1) * width] for i in range(4)])
        return lax.all_to_all(blocks, ROWS, 0, 0, tiled=True).reshape(4 * rows, width)

    def pack_pair(qkv_part, out_part):
        return jnp.concatenate([qkv_part, out_part.reshape(D // 4, -1)], axis=1)

    def split_pair(packed_part):
        return packed_part[:, : w_qkv.shape[2]], packed_part[:, w_qkv.shape[2] :].reshape(
            w_out.shape[1], -1
        )

    def fetch_attention(layer):
        near = swap_diagonal(pack_pair(w_qkv[layer], w_out[layer]))
        if layer == 0:
            half = near.shape[0] // 2
            by_x = swap_x(near)
            by_y = swap_y(near)
            corner = jnp.concatenate([swap_x(by_y[:half]), swap_y(by_x[half:])], axis=0)
            parts = [near, by_x, by_y, corner]
            parts = [jnp.where(column == 1, parts[i ^ 1], parts[i]) for i in range(4)]
            parts = [jnp.where(place >= 2, parts[i ^ 2], parts[i]) for i in range(4)]
        else:
            blocks = lax.all_gather(near, PLANE, axis=0)
            parts = [blocks[i] for i in range(4)]
        pairs = [split_pair(part) for part in parts]
        qkv_full = jnp.concatenate([pair[0] for pair in pairs], axis=0)
        out_full = jnp.concatenate([pair[1] for pair in pairs], axis=1)
        return qkv_full, out_full

    half_d = D // 8
    unit_half = share // 2
    parity = lax.axis_index(DP) % 2
    sources = [place ^ bits for bits in range(4)]
    zero, one = jnp.int32(0), jnp.int32(1)
    take_table = jnp.stack(
        [sources[0], sources[0], sources[1], sources[1], sources[2], sources[3]]
        + [zero, one, zero, one, parity, parity]
    ).astype(jnp.int32)
    put_table = jnp.stack(
        [sources[i // 2] for i in range(8)] + [zero, one] * 2 + [parity, 1 - parity] * 2
    ).astype(jnp.int32)
    table = jnp.concatenate([take_table, put_table])

    def block_of(i, s):
        return s[i]

    def half_of(i, s):
        return s[6 + i]

    def put_block(i, s):
        return s[12 + i]

    def put_half(i, s):
        return s[20 + i]

    def exchange(sent):
        core_part, y_part, corner_part = sent
        y_mine = xor_permute(y_part, 2)
        corner_mine = xor_permute(corner_part, 3)
        return (
            swap_core(core_part), y_mine, swap_group(y_mine), corner_mine, swap_group(corner_mine)
        )

    def moved(arrays, from_layer, block, source, bound_dim, bound, target, shape, dtype,
              layer=None, into=None):
        sent = take(arrays, table, from_layer, block, source, bound_dim, bound)
        parts = exchange(sent)
        return join(
            arrays, parts, table, from_layer, block, source, bound_dim, bound, target, shape,
            dtype, layer, into,
        )

    def fetch_wide(layer):
        return moved(
            (w_gate, w_up), layer, (half_d, share),
            lambda i, s: (half_of(i, s), block_of(i, s)), 1, units,
            lambda i, s: (2 * put_block(i, s) + put_half(i, s), 0), (D, share), bf16,
        )

    def fetch_narrow(layer):
        return moved(
            (w_down,), layer, (unit_half, D // 4),
            lambda i, s: (2 * block_of(i, s) + half_of(i, s), 0), 0, units,
            lambda i, s: (put_half(i, s), put_block(i, s)), (share, D), bf16,
        )[0]

    def give_wide(grad, layer, into):
        return moved(
            (grad,), None, (half_d, share),
            lambda i, s: (2 * block_of(i, s) + half_of(i, s), 0), 0, None,
            lambda i, s: (put_half(i, s), put_block(i, s)), w_gate.shape, f32, layer, into,
        )

    def give_narrow(grad, layer, into):
        return moved(
            (grad,), None, (unit_half, D // 4),
            lambda i, s: (half_of(i, s), block_of(i, s)), 0, None,
            lambda i, s: (2 * put_block(i, s) + put_half(i, s), 0), w_down.shape, f32, layer, into,
        )

    def return_wide(grad):
        blocks = grad.astype(bf16).reshape(4, D // 4, share)
        arrived = lax.all_to_all(blocks, ROWS, 0, 0, tiled=True)
        spread = jnp.concatenate([arrived[i] for i in range(4)], axis=1)[:, :units]
        return sum_dp(spread)

    def return_narrow(grad):
        rows = grad.astype(bf16)
        blocks = jnp.stack([rows[:, i * (D // 4) : (i + 1) * (D // 4)] for i in range(4)])
        arrived = lax.all_to_all(blocks, ROWS, 0, 0, tiled=True)
        spread = arrived.reshape(4 * share, -1)[:units]
        return sum_dp(spread)

    def return_attention(qkv_grad, out_grad_part):
        rows, columns = qkv_grad.astype(bf16), out_grad_part.astype(bf16)
        width = D // 4
        blocks = jnp.stack(
            [
                pack_pair(
                    rows[i * width : (i + 1) * width], columns[:, i * width : (i + 1) * width]
                )
                for i in range(4)
            ]
        )
        summed = lax.psum_scatter(blocks, PLANE)
        return split_pair(sum_dp(swap_diagonal(summed)))

    def all_tokens(values, by_line):
        mine = values[: values.shape[0] // 2]
        if by_line:
            near = gather_line(mine)
        else:
            near = lax.all_gather(mine, DP, axis=0, tiled=True)
        return near, swap_core(near)

    def mlp_weight_grads(normed, grads, gate_w, up_w, down_w):
        normed, grads, activated, grad_gate, grad_up = gated_all(
            normed, grads, gate_w, up_w, down_w
        )
        gate_grad = t_mm(normed, grad_gate).astype(bf16)
        up_grad = t_mm(normed, grad_up).astype(bf16)
        down_grad = t_mm(activated, grads).astype(bf16)
        return gate_grad, up_grad, down_grad

    both = tokens_whole(jnp.stack([hidden_in, out_grad]))
    resid = both[0].astype(f32)
    grad_start = both[1]
    own = resid.shape[0]

    saved = []
    for layer in range(LAYERS):
        qkv_full, out_full = fetch_attention(layer)
        gate_w, up_w = fetch_wide(layer)
        down_w = fetch_narrow(layer)
        normed_attn, scale_attn = norm_forward(resid, attn_gain_full[layer])
        pair_attn = jnp.concatenate([normed_attn, swap_core(normed_attn)], axis=0)
        qkv_rows = mm(pair_attn, qkv_full) + bias_here[layer][None, :]
        attended, kept = attention_forward(qkv_rows, frame)
        out_part = mm(attended, out_full)
        out_other = swap_core(out_part[own:].astype(bf16))
        middle = resid + out_part[:own] + out_other.astype(f32)
        normed_mlp, scale_mlp = norm_forward(middle, mlp_gain_full[layer])
        all_mlp = gather_eight(normed_mlp)
        gate = mm(all_mlp, gate_w)
        up = mm(all_mlp, up_w)
        activated = (jax.nn.silu(gate) * up).astype(bf16)
        saved.append(
            (resid, scale_attn, pair_attn, kept, attended, middle, scale_mlp, all_mlp, gate, up,
             activated, qkv_full, out_full, gate_w, up_w, down_w)
        )
        if layer < LAYERS - 1:
            resid = middle + scatter_eight(mm(activated, down_w))

    grad_resid = grad_start.astype(f32)
    grads = [None] * LAYERS
    small = [None] * LAYERS
    gate_out, up_out, narrow_out = None, None, None
    wide_parts, narrow_parts = [None] * LAYERS, [None] * LAYERS
    for layer in reversed(range(LAYERS)):
        (resid, scale_attn, pair_attn, kept, attended, middle, scale_mlp, all_mlp, gate, up,
         activated, qkv_full, out_full, gate_w, up_w, down_w) = saved[layer]
        all_grad = gather_eight(grad_resid.astype(bf16))
        if layer == 0:
            late = saved[LAYERS - 1]
            late_middle, late_units, _ = lax.optimization_barrier((late[5], late[10], all_grad))
            last_part = mm(late_units, late[15])
            resid_out = late_middle + scatter_eight(last_part)
            hidden_out = features_back(resid_out.astype(bf16))
        grad_units = mm_t(all_grad, down_w)
        _, grad_gate, grad_up = gated(gate, up, grad_units)
        grad_normed = scatter_eight(mm_t(grad_gate, gate_w) + mm_t(grad_up, up_w))
        if everyone:
            gate_grad, up_grad, down_grad = mlp_weight_grads(
                all_tokens(all_mlp, layer == LAYERS - 1),
                all_tokens(all_grad, layer < LAYERS - 1),
                gate_w, up_w, down_w,
            )
            narrow_out = give_narrow(down_grad, layer, narrow_out)
            gate_out = give_wide(gate_grad, layer, gate_out)
            up_out = give_wide(up_grad, layer, up_out)
        else:
            wide_parts[layer] = (
                return_wide(t_mm(all_mlp, grad_gate)),
                return_wide(t_mm(all_mlp, grad_up)),
            )
            narrow_parts[layer] = return_narrow(t_mm(activated, all_grad))
        grad_inner, mlp_gain_part = norm_backward(
            grad_normed, middle, scale_mlp, mlp_gain_full[layer]
        )
        grad_middle = grad_resid + grad_inner
        middle_round = grad_middle.astype(bf16)
        pair_grad = jnp.concatenate([middle_round, swap_core(middle_round)], axis=0)
        grad_heads = mm_t(pair_grad, out_full)
        out_grad_w = t_mm(attended, pair_grad)
        grad_qkv = attention_backward(grad_heads, kept, frame)
        bias_part = jnp.sum(grad_qkv, axis=0)
        qkv_round = grad_qkv.astype(bf16)
        grad_part = mm_t(qkv_round, qkv_full)
        grad_other = swap_core(grad_part[own:].astype(bf16))
        grad_normed_attn = grad_part[:own] + grad_other.astype(f32)
        qkv_grad_w = t_mm(pair_attn, qkv_round)
        grad_first, attn_gain_part = norm_backward(
            grad_normed_attn, resid, scale_attn, attn_gain_full[layer]
        )
        grad_resid = grad_middle + grad_first
        grads[layer] = return_attention(qkv_grad_w, out_grad_w)
        small[layer] = (attn_gain_part, mlp_gain_part, bias_part)
    in_grad = features_back(grad_resid.astype(bf16)).astype(f32)

    stacked = [
        jnp.stack([grads[layer][member].astype(f32) for layer in range(LAYERS)])
        for member in range(2)
    ]
    if everyone:
        stacked += [gate_out[0], up_out[0], narrow_out[0]]
    else:
        stacked += [
            jnp.stack([wide_parts[layer][member].astype(f32) for layer in range(LAYERS)])
            for member in range(2)
        ]
        stacked.append(jnp.stack([narrow_parts[layer].astype(f32) for layer in range(LAYERS)]))
    bias_stack = jnp.stack([small[layer][2] for layer in range(LAYERS)])
    bias_full = jnp.where(
        core == 0,
        jnp.concatenate([bias_stack, jnp.zeros_like(bias_stack)], axis=1),
        jnp.concatenate([jnp.zeros_like(bias_stack), bias_stack], axis=1),
    )
    packed = jnp.concatenate(
        [
            jnp.stack([small[layer][0] for layer in range(LAYERS)]),
            jnp.stack([small[layer][1] for layer in range(LAYERS)]),
            bias_full,
        ],
        axis=1,
    )
    packed = packed + swap_core(packed)
    packed = packed + swap_x(packed)
    packed = packed + swap_y(packed)
    if everyone:
        packed = sum_dp(packed)
    else:
        packed = lax.psum(packed, DP)
    row_width = attn_gain.shape[1]
    col_width = b_qkv.shape[1]
    row_place = place * row_width
    attn_gain_grad = lax.dynamic_slice_in_dim(packed[:, :D], row_place, row_width, 1)
    mlp_gain_grad = lax.dynamic_slice_in_dim(packed[:, D : 2 * D], row_place, row_width, 1)
    bias_grad = lax.dynamic_slice_in_dim(packed[:, 2 * D :], column * col_width, col_width, 1)
    return (
        hidden_out,
        in_grad,
        attn_gain_grad,
        stacked[0],
        bias_grad,
        stacked[1],
        mlp_gain_grad,
        stacked[2],
        stacked[3],
        stacked[4],
    )


def solution(mesh):
    fine = Mesh(
        mesh.devices.reshape(mesh.shape["dp"], 2, mesh.shape["rows"] // 2, mesh.shape["cols"]),
        (DP, RY, RK, CX),
    )
    in_specs = (
        P((DP, CX), ROWS),
        P(None, ROWS),
        P(None, ROWS, CX),
        P(None, CX),
        P(None, CX, ROWS),
        P(None, ROWS),
        P(None, ROWS, CX),
        P(None, ROWS, CX),
        P(None, CX, ROWS),
        P((DP, CX), ROWS),
    )
    out_specs = (
        P((DP, CX), ROWS),
        P((DP, CX), ROWS),
        P(None, ROWS),
        P(None, ROWS, CX),
        P(None, CX),
        P(None, CX, ROWS),
        P(None, ROWS),
        P(None, ROWS, CX),
        P(None, ROWS, CX),
        P(None, CX, ROWS),
    )

    return jax.shard_map(body, mesh=fine, in_specs=in_specs, out_specs=out_specs, check_vma=False)
```
